256 devices in a mesh: row: 16 (over y, x), col: 16 (over z, core).
Axes of the slice: x: 4, y: 4, z: 8, core: 2. Of those that a mesh axis runs over, the one named last changes fastest.
Arguments:
- flow_tiles: float32 [24576, 24576], P('row', 'col'), may hold values from 1 to 40
- anchor: float32 [48, 24576], P(None, 'row'), may hold values from 0.2 to 2
- destination: float32 [48, 24576], P(None, 'col'), may hold values from 0.2 to 2
Outputs:
- anchor_new: float32 [48, 24576], P(None, 'row')
- destination_new: float32 [48, 24576], P(None, 'col')
The draws below stay inside these ranges and needn't reach their ends.
All inputs are finite; a program needn't handle non-finite values.
Results may differ from the reference program's by a relative error of at most 0.00011.
Values sent between devices are 32-bit elements; how exact they have to be, the bound alone decides.
No kernel may reach another device: no remote copies, remote signals or barrier semaphores. Data moves between devices by JAX's collectives and lax.ppermute only.
A program may use at most 64 MiB of HBM per device.

```python
import math
import jax
import jax.numpy as jnp
from jax import lax

RANK = 48
SPAN = 96
ITERS = 2
ZONES = 24576
N_ROW = 16
N_COL = 16


def block_levels(own_key, extent, cuts, low, top_value):
    loudness, own = 1.0, jax.random.fold_in(own_key, 6)
    for dim, blocks in cuts:
        draws = jnp.exp(jax.random.uniform(jax.random.fold_in(own, dim), (blocks,), jnp.float32, low / len(cuts), top_value / len(cuts)))
        loudness = loudness * jnp.repeat(draws, extent[dim] // blocks).reshape([-1 if axis == dim else 1 for axis in range(len(extent))])
    return loudness


def setup_inputs(seed: int = 0) -> dict:
    streams_of = jax.random.split(jax.random.key(seed), 4)
    flow_tiles = jnp.clip(jnp.exp(math.log(40.0) - 3.6888795 * jax.random.uniform(streams_of[0], (ZONES, ZONES), jnp.float32) ** block_levels(streams_of[0], (ZONES, ZONES), ((0, 16), (1, 16)), -0.2, 0.2)), 1.0, 40.0)
    anchor = jnp.clip(jnp.exp(math.log(2.0) - 2.3025851 * jax.random.uniform(streams_of[1], (RANK, ZONES), jnp.float32) ** block_levels(streams_of[1], (RANK, ZONES), ((1, 16),), -0.2, 0.2)), 0.2, 2.0)
    destination = jnp.clip(jnp.exp(math.log(2.0) - 2.3025851 * jax.random.uniform(streams_of[2], (RANK, ZONES), jnp.float32) ** block_levels(streams_of[2], (RANK, ZONES), ((1, 16),), -0.2, 0.2)), 0.2, 2.0)
    return dict(flow_tiles=flow_tiles, anchor=anchor, destination=destination)


HIGH = lax.Precision.HIGHEST


def contract(left, right, dims):
    return lax.dot_general(left, right, (dims, ((), ())), precision=HIGH, preferred_element_type=jnp.float32)


def anchor_half(flow_tiles, anchor, destination):
    blocks = N_ROW * N_COL
    flow_blocks = flow_tiles.reshape(blocks, SPAN, ZONES)
    anchor_blocks = anchor.reshape(RANK, blocks, SPAN).transpose(1, 0, 2)

    def one_block(pieces):
        flow_part, anchor_part = pieces
        rebuilt = contract(anchor_part, destination, ((0,), (0,)))
        ratios = flow_part / rebuilt
        return contract(destination, ratios, ((1,), (1,)))

    numerator = lax.map(one_block, (flow_blocks, anchor_blocks))
    numerator = numerator.transpose(1, 0, 2).reshape(RANK, ZONES)
    totals = jnp.sum(destination, axis=1)
    return anchor * numerator / totals[:, None]


def destination_half(flow_tiles, anchor, destination):
    blocks = N_ROW * N_COL
    flow_blocks = flow_tiles.reshape(blocks, SPAN, ZONES)
    anchor_blocks = anchor.reshape(RANK, blocks, SPAN).transpose(1, 0, 2)

    def one_block(summed, pieces):
        flow_part, anchor_part = pieces
        rebuilt = contract(anchor_part, destination, ((0,), (0,)))
        ratios = flow_part / rebuilt
        return summed + contract(anchor_part, ratios, ((1,), (0,))), None

    start = jnp.zeros((RANK, ZONES), jnp.float32)
    numerator, _ = lax.scan(one_block, start, (flow_blocks, anchor_blocks))
    totals = jnp.sum(anchor, axis=1)
    return destination * numerator / totals[:, None]


def reference(flow_tiles, anchor, destination):
    for sweep_index in range(ITERS):
        anchor = anchor_half(flow_tiles, anchor, destination)
        destination = destination_half(flow_tiles, anchor, destination)
    return anchor, destination
```

```python
import functools

import jax
import jax.numpy as jnp
from jax import lax
from jax.experimental import pallas as pl
from jax.experimental.pallas import tpu as pltpu
from jax.sharding import PartitionSpec as P

ITERS = 2
RANK = 48
LANES = 128
COLS = 256
ROWS = 256

F32 = jnp.float32
BF16 = jnp.bfloat16

PIECE = 40


def split(x):
    high = x.astype(BF16)
    return high, (x - high.astype(F32)).astype(BF16)


def load_tile(ref, natural, part, tile, peers):
    if natural:
        return ref[part * peers : (part + 1) * peers, tile * LANES : (tile + 1) * LANES]
    tiles = 12
    return ref[pl.ds(part * tiles + tile, peers, stride=PIECE), :]


def store_pieces(out_ref, total, sums, peers):
    tiles = total.shape[1] // LANES
    parts = RANK // peers
    for part in range(parts):
        rows = slice(part * peers, (part + 1) * peers)
        for tile in range(tiles):
            out_ref[pl.ds(part * tiles + tile, peers, stride=PIECE), :] = total[
                rows, tile * LANES : (tile + 1) * LANES
            ]
        out_ref[pl.ds(parts * tiles + part, peers, stride=PIECE), :] = sums[rows]
    out_ref[pl.ds(parts * tiles + parts, peers, stride=PIECE), :] = jnp.zeros((peers, LANES), F32)


def half_kernel(
    kind, peers, nat_a, nat_d, emit_a, flow_hbm, a_ref, d_ref, out_ref, *rest
):
    if emit_a:
        a_out, *rest = rest
    a_f, a_t, a_cat, d_w, d_cat, acc, acc_t, *rest = rest
    flow, sem = rest
    zones_i, zones_j = flow.shape
    steps = zones_j // COLS
    parts = RANK // peers

    def fetch(step):
        at = pl.ds(step * COLS, COLS)
        return pltpu.make_async_copy(flow_hbm.at[:, at], flow.at[:, at], sem.at[step])

    for step in range(steps):
        fetch(step).start()

    sums = []
    for part in range(parts):
        total = None
        low = part * peers
        for tile in range(zones_j // LANES):
            at = slice(tile * LANES, (tile + 1) * LANES)
            x = load_tile(d_ref, nat_d, part, tile, peers)
            high, rest_x = split(x)
            for base in (0, 64):
                d_w[base + low : base + low + peers, at] = high
                d_w[128 + base + low : 128 + base + low + peers, at] = rest_x
            d_cat[low : low + peers, at] = high
            d_cat[RANK + low : RANK + low + peers, at] = rest_x
            if kind == "anchor":
                total = x if total is None else total + x
        for tile in range(zones_i // LANES):
            at = slice(tile * LANES, (tile + 1) * LANES)
            x = load_tile(a_ref, nat_a, part, tile, peers)
            high, rest_x = split(x)
            a_f[low : low + peers, at] = high.astype(F32)
            a_f[64 + low : 64 + low + peers, at] = rest_x.astype(F32)
            if kind == "destination":
                a_cat[low : low + peers, at] = high
                a_cat[RANK + low : RANK + low + peers, at] = rest_x
                total = x if total is None else total + x
            if emit_a:
                a_out[low : low + peers, at] = x
        sums.append(total)
    sums = jnp.concatenate(sums, axis=0)
    gap = jnp.zeros((16, zones_j), BF16)
    for base in (0, 64, 128, 192):
        d_w[base + RANK : base + 64, :] = gap
    gap = jnp.zeros((16, zones_i), F32)
    for base in (0, 64):
        a_f[base + RANK : base + 64, :] = gap
    for tile in range(zones_i // LANES):
        at = slice(tile * LANES, (tile + 1) * LANES)
        x = a_f[:, at].T.astype(BF16)
        a_t[at, :LANES] = x
        a_t[at, LANES:] = x

    if kind == "anchor":
        acc_t[...] = jnp.zeros_like(acc_t)

    def step_body(step, carry):
        fetch(step).wait()
        at = pl.ds(pl.multiple_of(step * COLS, COLS), COLS)
        weights = d_w[:, at]
        total = None
        for block in range(zones_i // ROWS):
            rows = slice(block * ROWS, (block + 1) * ROWS)
            rebuilt = jnp.dot(a_t[rows, :], weights, preferred_element_type=F32)
            piece = flow[rows, at]
            inverse = pl.reciprocal(rebuilt, approx=True)
            first = (piece * inverse).astype(BF16)
            second = ((piece - rebuilt * first.astype(F32)) * inverse).astype(BF16)
            if kind == "anchor":
                right = d_cat[:, at]
                dims = (((1,), (1,)), ((), ()))
                acc_t[rows, : 2 * RANK] += lax.dot_general(
                    first, right, dims, preferred_element_type=F32
                ) + lax.dot_general(second, right, dims, preferred_element_type=F32)
            else:
                left = a_cat[:, rows]
                term = jnp.dot(left, first, preferred_element_type=F32) + jnp.dot(
                    left, second, preferred_element_type=F32
                )
                total = term if total is None else total + term
        if kind == "destination":
            acc[:, at] = total[:RANK] + total[RANK:]
        return carry

    lax.fori_loop(0, steps, step_body, 0)

    if kind == "anchor":
        for tile in range(zones_i // LANES):
            at = slice(tile * LANES, (tile + 1) * LANES)
            x = acc_t[at, :].T
            acc[:, at] = x[:RANK] + x[RANK : 2 * RANK]
    store_pieces(out_ref, acc, sums, peers)


def half(kind, peers, flow, a, d, emit_a=False):
    zones_i, zones_j = flow.shape
    nat_a, nat_d = a.shape[0] == RANK, d.shape[0] == RANK
    out_shape = [jax.ShapeDtypeStruct((peers * PIECE, LANES), F32)]
    if emit_a:
        out_shape.append(jax.ShapeDtypeStruct((RANK, zones_i), F32))
    vmem = pl.BlockSpec(memory_space=pltpu.VMEM)
    own = [pltpu.VMEM((zones_i, zones_j), F32), pltpu.SemaphoreType.DMA((zones_j // COLS,))]
    out = pl.pallas_call(
        functools.partial(half_kernel, kind, peers, nat_a, nat_d, emit_a),
        out_shape=out_shape,
        in_specs=[pl.BlockSpec(memory_space=pl.ANY), vmem, vmem],
        out_specs=[vmem] * len(out_shape),
        scratch_shapes=[
            pltpu.VMEM((LANES, zones_i), F32),
            pltpu.VMEM((zones_i, 2 * LANES), BF16),
            pltpu.VMEM((2 * RANK, zones_i), BF16),
            pltpu.VMEM((2 * LANES, zones_j), BF16),
            pltpu.VMEM((2 * RANK, zones_j), BF16),
            pltpu.VMEM((RANK, zones_i), F32),
            pltpu.VMEM((zones_i, LANES), F32),
            *own,
        ],
        compiler_params=pltpu.CompilerParams(vmem_limit_bytes=32 * 2**20),
        name="half_" + kind,
    )(pltpu.with_memory_space_constraint(flow, pltpu.HBM), a, d)
    return out if emit_a else out[0]


def update_kernel(axis, peers, natural, got_ref, old_ref, out_ref, old):
    me = lax.axis_index(axis)
    parts = RANK // peers
    if natural:
        tiles = old_ref.shape[1] // LANES
        for part in range(parts):
            x = old_ref[part * peers : (part + 1) * peers, :]
            mine = lax.broadcasted_iota(jnp.int32, x.shape, 0) == me
            x = jnp.sum(jnp.where(mine, x, 0.0), axis=0, keepdims=True)
            for tile in range(tiles):
                row = part * tiles + tile
                old[row : row + 1, :] = x[:, tile * LANES : (tile + 1) * LANES]
        old[parts * tiles :, :] = jnp.zeros((PIECE - parts * tiles, LANES), F32)
        before = old[...]
    else:
        before = old_ref[pl.ds(pl.multiple_of(me * PIECE, 8), PIECE), :]
        tiles = 12
    total = got_ref[:PIECE, :]
    for peer in range(1, peers):
        total = total + got_ref[peer * PIECE : (peer + 1) * PIECE, :]
    row = lax.broadcasted_iota(jnp.int32, (PIECE, LANES), 0)
    norm = jnp.zeros((PIECE, LANES), F32)
    for part in range(parts):
        at = parts * tiles + part
        norm = jnp.where(row >= part * tiles, jnp.sum(total[at : at + 1, :]), norm)
    new = jnp.where(row < parts * tiles, before * total / norm, 0.0)
    for peer in range(peers):
        out_ref[peer * PIECE : (peer + 1) * PIECE, :] = new


def update(axis, peers, got, old):
    vmem = pl.BlockSpec(memory_space=pltpu.VMEM)
    return pl.pallas_call(
        functools.partial(update_kernel, axis, peers, old.shape[0] == RANK),
        out_shape=jax.ShapeDtypeStruct((peers * PIECE, LANES), F32),
        in_specs=[vmem, vmem],
        out_specs=vmem,
        scratch_shapes=[pltpu.VMEM((PIECE, LANES), F32)],
        compiler_params=pltpu.CompilerParams(vmem_limit_bytes=4 * 2**20),
        name="update",
    )(got, old)


def whole_kernel(peers, in_ref, out_ref):
    for part in range(RANK // peers):
        for tile in range(out_ref.shape[1] // LANES):
            out_ref[part * peers : (part + 1) * peers, tile * LANES : (tile + 1) * LANES] = load_tile(
                in_ref, False, part, tile, peers
            )


def whole(peers, pieces, zones):
    vmem = pl.BlockSpec(memory_space=pltpu.VMEM)
    return pl.pallas_call(
        functools.partial(whole_kernel, peers),
        out_shape=jax.ShapeDtypeStruct((RANK, zones), F32),
        in_specs=[vmem],
        out_specs=vmem,
        compiler_params=pltpu.CompilerParams(vmem_limit_bytes=4 * 2**20),
        name="whole",
    )(pieces)


def exchange(x, axis):
    return lax.all_to_all(x, axis, 0, 0, tiled=True)


def body(n_row, n_col, flow, anchor, destination):
    anchor_out = None
    for sweep in range(ITERS):
        sent = half("anchor", n_col, flow, anchor, destination)
        sent = update("col", n_col, exchange(sent, "col"), anchor)
        anchor = exchange(sent, "col")
        last = sweep == ITERS - 1
        sent = half("destination", n_row, flow, anchor, destination, emit_a=last)
        if last:
            sent, anchor_out = sent
        sent = update("row", n_row, exchange(sent, "row"), destination)
        destination = exchange(sent, "row")
    return anchor_out, whole(n_row, destination, flow.shape[1])


def solution(mesh):
    n_row, n_col = mesh.shape["row"], mesh.shape["col"]
    in_specs = (P("row", "col"), P(None, "row"), P(None, "col"))
    out_specs = (P(None, "row"), P(None, "col"))
    return jax.shard_map(
        functools.partial(body, n_row, n_col),
        mesh=mesh,
        in_specs=in_specs,
        out_specs=out_specs,
        check_vma=False,
    )
```

```python
import functools

import jax
import jax.numpy as jnp
from jax import lax
from jax.experimental import pallas as pl
from jax.experimental.pallas import tpu as pltpu
from jax.sharding import PartitionSpec as P

ITERS = 2
RANK = 48
LANES = 128
COLS = 256
ROWS = 256

F32 = jnp.float32
BF16 = jnp.bfloat16

PIECE = 40


def split(x):
    high = x.astype(BF16)
    return high, (x - high.astype(F32)).astype(BF16)


def load_tile(ref, natural, part, tile, peers):
    if natural:
        return ref[part * peers : (part + 1) * peers, tile * LANES : (tile + 1) * LANES]
    tiles = 12
    return ref[pl.ds(part * tiles + tile, peers, stride=PIECE), :]


def store_pieces(out_ref, total, sums, peers):
    tiles = total.shape[1] // LANES
    parts = RANK // peers
    for part in range(parts):
        rows = slice(part * peers, (part + 1) * peers)
        for tile in range(tiles):
            out_ref[pl.ds(part * tiles + tile, peers, stride=PIECE), :] = total[
                rows, tile * LANES : (tile + 1) * LANES
            ]
        out_ref[pl.ds(parts * tiles + part, peers, stride=PIECE), :] = sums[rows]
    out_ref[pl.ds(parts * tiles + parts, peers, stride=PIECE), :] = jnp.zeros((peers, LANES), F32)


def half_kernel(kind, peers, nat_u, nat_v, emit_v, first, flow_in, u_ref, v_ref, out_ref, *rest):
    rest = list(rest)
    v_out = rest.pop(0) if emit_v else None
    flow = rest.pop(0) if first else flow_in
    v_f, v_t, v_cat, u_w, acc, *sem = rest
    zones_u, zones_v = u_w.shape[1], v_t.shape[0]
    steps = zones_u // COLS
    parts = RANK // peers

    def fetch(step):
        at = pl.ds(step * COLS, COLS)
        where = (at, slice(None)) if kind == "anchor" else (slice(None), at)
        return pltpu.make_async_copy(flow_in.at[where], flow.at[where], sem[0].at[step])

    if first:
        for step in range(steps):
            fetch(step).start()

    sums = []
    for part in range(parts):
        total = None
        low = part * peers
        for tile in range(zones_u // LANES):
            at = slice(tile * LANES, (tile + 1) * LANES)
            high, low_term = split(load_tile(u_ref, nat_u, part, tile, peers))
            for base in (0, 64):
                u_w[base + low : base + low + peers, at] = high
                u_w[128 + base + low : 128 + base + low + peers, at] = low_term
        for tile in range(zones_v // LANES):
            at = slice(tile * LANES, (tile + 1) * LANES)
            x = load_tile(v_ref, nat_v, part, tile, peers)
            high, low_term = split(x)
            v_f[low : low + peers, at] = high.astype(F32)
            v_f[64 + low : 64 + low + peers, at] = low_term.astype(F32)
            v_cat[low : low + peers, at] = high
            v_cat[RANK + low : RANK + low + peers, at] = low_term
            total = x if total is None else total + x
            if emit_v:
                v_out[low : low + peers, at] = x
        sums.append(total)
    sums = jnp.concatenate(sums, axis=0)
    gap = jnp.zeros((16, zones_u), BF16)
    for base in (0, 64, 128, 192):
        u_w[base + RANK : base + 64, :] = gap
    gap = jnp.zeros((16, zones_v), F32)
    for base in (0, 64):
        v_f[base + RANK : base + 64, :] = gap
    for tile in range(zones_v // LANES):
        at = slice(tile * LANES, (tile + 1) * LANES)
        x = v_f[:, at].T.astype(BF16)
        v_t[at, :LANES] = x
        v_t[at, LANES:] = x

    def step_body(step, carry):
        if first:
            fetch(step).wait()
        at = pl.ds(pl.multiple_of(step * COLS, COLS), COLS)
        weights = u_w[:, at]
        total = None
        for block in range(zones_v // ROWS):
            rows = slice(block * ROWS, (block + 1) * ROWS)
            rebuilt = jnp.dot(v_t[rows, :], weights, preferred_element_type=F32)
            piece = flow[at, rows].T if kind == "anchor" else flow[rows, at]
            inverse = pl.reciprocal(rebuilt, approx=True)
            head = (piece * inverse).astype(BF16)
            tail = ((piece - rebuilt * head.astype(F32)) * inverse).astype(BF16)
            left = v_cat[:, rows]
            term = jnp.dot(left, head, preferred_element_type=F32)
            term += jnp.dot(left, tail, preferred_element_type=F32)
            total = term if total is None else total + term
        acc[:, at] = total[:RANK] + total[RANK:]
        return carry

    lax.fori_loop(0, steps, step_body, 0)
    store_pieces(out_ref, acc, sums, peers)


def half(kind, peers, flow, u, v, emit_v=False, first=False):
    zones_u, zones_v = flow.shape if kind == "anchor" else flow.shape[::-1]
    nat_u, nat_v = u.shape[0] == RANK, v.shape[0] == RANK
    vmem = pl.BlockSpec(memory_space=pltpu.VMEM)
    out_shape = [jax.ShapeDtypeStruct((peers * PIECE, LANES), F32)]
    if emit_v:
        out_shape.append(jax.ShapeDtypeStruct((RANK, zones_v), F32))
    if first:
        out_shape.append(pltpu.VMEM(flow.shape, F32))
        flow = pltpu.with_memory_space_constraint(flow, pltpu.HBM)
    return pl.pallas_call(
        functools.partial(half_kernel, kind, peers, nat_u, nat_v, emit_v, first),
        out_shape=out_shape,
        in_specs=[pl.BlockSpec(memory_space=pl.ANY) if first else vmem, vmem, vmem],
        out_specs=[vmem] * len(out_shape),
        scratch_shapes=[
            pltpu.VMEM((LANES, zones_v), F32),
            pltpu.VMEM((zones_v, 2 * LANES), BF16),
            pltpu.VMEM((2 * RANK, zones_v), BF16),
            pltpu.VMEM((2 * LANES, zones_u), BF16),
            pltpu.VMEM((RANK, zones_u), F32),
            *([pltpu.SemaphoreType.DMA((zones_u // COLS,))] if first else []),
        ],
        compiler_params=pltpu.CompilerParams(vmem_limit_bytes=30 * 2**20),
        name="half_" + kind,
    )(flow, u, v)


def update_kernel(axis, peers, natural, got_ref, old_ref, out_ref, old):
    me = lax.axis_index(axis)
    parts = RANK // peers
    if natural:
        tiles = old_ref.shape[1] // LANES
        for part in range(parts):
            x = old_ref[part * peers : (part + 1) * peers, :]
            mine = lax.broadcasted_iota(jnp.int32, x.shape, 0) == me
            x = jnp.sum(jnp.where(mine, x, 0.0), axis=0, keepdims=True)
            for tile in range(tiles):
                row = part * tiles + tile
                old[row : row + 1, :] = x[:, tile * LANES : (tile + 1) * LANES]
        old[parts * tiles :, :] = jnp.zeros((PIECE - parts * tiles, LANES), F32)
        before = old[...]
    else:
        before = old_ref[pl.ds(pl.multiple_of(me * PIECE, 8), PIECE), :]
        tiles = 12
    total = got_ref[:PIECE, :]
    for peer in range(1, peers):
        total = total + got_ref[peer * PIECE : (peer + 1) * PIECE, :]
    row = lax.broadcasted_iota(jnp.int32, (PIECE, LANES), 0)
    norm = jnp.zeros((PIECE, LANES), F32)
    for part in range(parts):
        at = parts * tiles + part
        norm = jnp.where(row >= part * tiles, jnp.sum(total[at : at + 1, :]), norm)
    new = jnp.where(row < parts * tiles, before * total / norm, 0.0)
    for peer in range(peers):
        out_ref[peer * PIECE : (peer + 1) * PIECE, :] = new


def update(axis, peers, got, old):
    vmem = pl.BlockSpec(memory_space=pltpu.VMEM)
    return pl.pallas_call(
        functools.partial(update_kernel, axis, peers, old.shape[0] == RANK),
        out_shape=jax.ShapeDtypeStruct((peers * PIECE, LANES), F32),
        in_specs=[vmem, vmem],
        out_specs=vmem,
        scratch_shapes=[pltpu.VMEM((PIECE, LANES), F32)],
        compiler_params=pltpu.CompilerParams(vmem_limit_bytes=4 * 2**20),
        name="update",
    )(got, old)


def whole_kernel(peers, in_ref, out_ref):
    for part in range(RANK // peers):
        for tile in range(out_ref.shape[1] // LANES):
            out_ref[part * peers : (part + 1) * peers, tile * LANES : (tile + 1) * LANES] = load_tile(
                in_ref, False, part, tile, peers
            )


def whole(peers, pieces, zones):
    vmem = pl.BlockSpec(memory_space=pltpu.VMEM)
    return pl.pallas_call(
        functools.partial(whole_kernel, peers),
        out_shape=jax.ShapeDtypeStruct((RANK, zones), F32),
        in_specs=[vmem],
        out_specs=vmem,
        compiler_params=pltpu.CompilerParams(vmem_limit_bytes=4 * 2**20),
        name="whole",
    )(pieces)


def exchange(x, axis):
    return lax.all_to_all(x, axis, 0, 0, tiled=True)


def body(n_row, n_col, flow, anchor, destination):
    anchor_out = None
    for sweep in range(ITERS):
        if sweep == 0:
            sent, flow = half("anchor", n_col, flow, anchor, destination, first=True)
        else:
            (sent,) = half("anchor", n_col, flow, anchor, destination)
        sent = update("col", n_col, exchange(sent, "col"), anchor)
        anchor = exchange(sent, "col")
        last = sweep == ITERS - 1
        sent, *rest = half("destination", n_row, flow, destination, anchor, emit_v=last)
        if last:
            (anchor_out,) = rest
        sent = update("row", n_row, exchange(sent, "row"), destination)
        destination = exchange(sent, "row")
    return anchor_out, whole(n_row, destination, flow.shape[1])


def solution(mesh):
    n_row, n_col = mesh.shape["row"], mesh.shape["col"]
    in_specs = (P("row", "col"), P(None, "row"), P(None, "col"))
    out_specs = (P(None, "row"), P(None, "col"))
    return jax.shard_map(
        functools.partial(body, n_row, n_col),
        mesh=mesh,
        in_specs=in_specs,
        out_specs=out_specs,
        check_vma=False,
    )
```

```python
import functools

import jax
import jax.numpy as jnp
from jax import lax
from jax.experimental import pallas as pl
from jax.experimental.pallas import tpu as pltpu
from jax.sharding import PartitionSpec as P

ITERS = 2
RANK = 48
LANES = 128
COLS = 256
ROWS = 256

F32 = jnp.float32
BF16 = jnp.bfloat16

PART = 16
PARTS = RANK // PART

PIECE = 40
TILES = 12
VMEM = pl.BlockSpec(memory_space=pltpu.VMEM)


def split(x):
    high = x.astype(BF16)
    return high, (x - high.astype(F32)).astype(BF16)


def swap(core, mine, other):
    return jnp.where(core == 0, mine, other), jnp.where(core == 0, other, mine)


def load_tile(refs, core, part, tile):
    if refs[0].shape[0] == RANK:
        return refs[0][part * PART : (part + 1) * PART, tile * LANES : (tile + 1) * LANES]
    row = part * TILES + tile
    if len(refs) == 1:
        return refs[0][pl.ds(row, PART, stride=PIECE), :]
    half_part = [ref[pl.ds(row, PART // 2, stride=PIECE), :] for ref in refs]
    return jnp.concatenate(swap(core, *half_part), axis=0)


def store_rows(refs, core, row, x):
    if len(refs) == 1:
        refs[0][pl.ds(row, PART, stride=PIECE), :] = x
    else:
        for ref, y in zip(refs, swap(core, x[: PART // 2], x[PART // 2 :])):
            ref[pl.ds(row, PART // 2, stride=PIECE), :] = y


def half_kernel(kind, n_u, n_v, n_out, emit_v, first, *refs):
    refs = list(refs)
    take = lambda n: [refs.pop(0) for _ in range(n)]
    (flow_in,), u_refs, v_refs, out_refs = take(1), take(n_u), take(n_v), take(n_out)
    (v_out,) = take(1) if emit_v else (None,)
    (flow,) = take(1) if first else (flow_in,)
    v_f, v_t, v_cat, u_w, acc = take(5)
    zones_u, zones_v = u_w.shape[1], v_t.shape[0]
    steps = zones_u // COLS
    core = lax.rem(lax.axis_index("col"), 2)

    def fetch(step):
        at = pl.ds(step * COLS, COLS)
        where = (at, slice(None)) if kind == "anchor" else (slice(None), at)
        return pltpu.make_async_copy(flow_in.at[where], flow.at[where], sem.at[step])

    if first:
        u_buf, v_buf, sem, factor_sem = refs
        copies = [
            pltpu.make_async_copy(u_refs[0], u_buf, factor_sem.at[0]),
            pltpu.make_async_copy(v_refs[0], v_buf, factor_sem.at[1]),
        ]
        for copy in copies:
            copy.start()
        fetch(0).start()
        for copy in copies:
            copy.wait()
        fetch(1).start()
        u_refs, v_refs = [u_buf], [v_buf]

    sums = []
    for part in range(PARTS):
        total = None
        low = part * PART
        for tile in range(zones_u // LANES):
            at = slice(tile * LANES, (tile + 1) * LANES)
            high, low_term = split(load_tile(u_refs, core, part, tile))
            for base in (0, 64):
                u_w[base + low : base + low + PART, at] = high
                u_w[128 + base + low : 128 + base + low + PART, at] = low_term
        for tile in range(zones_v // LANES):
            at = slice(tile * LANES, (tile + 1) * LANES)
            x = load_tile(v_refs, core, part, tile)
            high, low_term = split(x)
            v_f[low : low + PART, at] = high.astype(F32)
            v_f[64 + low : 64 + low + PART, at] = low_term.astype(F32)
            v_cat[low : low + PART, at] = high
            v_cat[RANK + low : RANK + low + PART, at] = low_term
            total = x if total is None else total + x
            if emit_v:
                v_out[low : low + PART, at] = x
        sums.append(total)
    gap = jnp.zeros((16, zones_u), BF16)
    for base in (0, 64, 128, 192):
        u_w[base + RANK : base + 64, :] = gap
    gap = jnp.zeros((16, zones_v), F32)
    for base in (0, 64):
        v_f[base + RANK : base + 64, :] = gap
    for tile in range(zones_v // LANES):
        at = slice(tile * LANES, (tile + 1) * LANES)
        x = v_f[:, at].T.astype(BF16)
        v_t[at, :LANES] = x
        v_t[at, LANES:] = x

    def step_body(step, carry):
        if first:
            fetch(step).wait()

            @pl.when(step + 2 < steps)
            def _():
                fetch(step + 2).start()

        at = pl.ds(pl.multiple_of(step * COLS, COLS), COLS)
        weights = u_w[:, at]
        total = None
        for block in range(zones_v // ROWS):
            rows = slice(block * ROWS, (block + 1) * ROWS)
            rebuilt = jnp.dot(v_t[rows, :], weights, preferred_element_type=F32)
            piece = flow[at, rows].T if kind == "anchor" else flow[rows, at]
            inverse = pl.reciprocal(rebuilt, approx=True)
            head = (piece * inverse).astype(BF16)
            tail = ((piece - rebuilt * head.astype(F32)) * inverse).astype(BF16)
            left = v_cat[:, rows]
            term = jnp.dot(left, head, preferred_element_type=F32)
            term += jnp.dot(left, tail, preferred_element_type=F32)
            total = term if total is None else total + term
        acc[:, at] = total[:RANK] + total[RANK:]
        return carry

    lax.fori_loop(0, steps, step_body, 0)

    for part in range(PARTS):
        ranks = slice(part * PART, (part + 1) * PART)
        for tile in range(TILES):
            x = acc[ranks, tile * LANES : (tile + 1) * LANES]
            store_rows(out_refs, core, part * TILES + tile, x)
        store_rows(out_refs, core, PARTS * TILES + part, sums[part])
    store_rows(out_refs, core, PARTS * TILES + PARTS, jnp.zeros((PART, LANES), F32))


def half(kind, flow, u, v, emit_v=False, first=False):
    zones_u, zones_v = flow.shape if kind == "anchor" else flow.shape[::-1]
    n_out = 2 if kind == "anchor" else 1
    out_shape = [jax.ShapeDtypeStruct((PART // n_out * PIECE, LANES), F32)] * n_out
    if emit_v:
        out_shape.append(jax.ShapeDtypeStruct((RANK, zones_v), F32))
    scratch = [
        pltpu.VMEM((LANES, zones_v), F32),
        pltpu.VMEM((zones_v, 2 * LANES), BF16),
        pltpu.VMEM((2 * RANK, zones_v), BF16),
        pltpu.VMEM((2 * LANES, zones_u), BF16),
        pltpu.VMEM((RANK, zones_u), F32),
    ]
    operands = [flow, *u, *v]
    if first:
        out_shape.append(pltpu.VMEM(flow.shape, F32))
        operands = [pltpu.with_memory_space_constraint(x, pltpu.HBM) for x in operands]
        scratch += [
            pltpu.VMEM((RANK, zones_u), F32),
            pltpu.VMEM((RANK, zones_v), F32),
            pltpu.SemaphoreType.DMA((zones_u // COLS,)),
            pltpu.SemaphoreType.DMA((2,)),
        ]
    return pl.pallas_call(
        functools.partial(half_kernel, kind, len(u), len(v), n_out, emit_v, first),
        out_shape=out_shape,
        in_specs=[pl.BlockSpec(memory_space=pl.ANY) if first else VMEM] * len(operands),
        out_specs=[VMEM] * len(out_shape),
        scratch_shapes=scratch,
        compiler_params=pltpu.CompilerParams(vmem_limit_bytes=30 * 2**20),
        name="half_" + kind,
    )(*operands)


def update_kernel(axis, peers, got_ref, old_ref, out_ref, old):
    me = lax.axis_index(axis)
    if axis == "col":
        slot, core = me // 2, lax.rem(me, 2)
        me = core * (PART // 2) + slot
    else:
        slot = me
    if old_ref.shape[0] == RANK:
        for part in range(PARTS):
            x = old_ref[part * PART : (part + 1) * PART, :]
            mine = lax.broadcasted_iota(jnp.int32, x.shape, 0) == me
            x = jnp.sum(jnp.where(mine, x, 0.0), axis=0, keepdims=True)
            for tile in range(TILES):
                row = part * TILES + tile
                old[row : row + 1, :] = x[:, tile * LANES : (tile + 1) * LANES]
        old[PARTS * TILES :, :] = jnp.zeros((PIECE - PARTS * TILES, LANES), F32)
        before = old[...]
    else:
        before = old_ref[pl.ds(pl.multiple_of(slot * PIECE, 8), PIECE), :]
    total = got_ref[:PIECE, :]
    for peer in range(1, peers):
        total = total + got_ref[peer * PIECE : (peer + 1) * PIECE, :]
    row = lax.broadcasted_iota(jnp.int32, (PIECE, LANES), 0)
    norm = jnp.zeros((PIECE, LANES), F32)
    for part in range(PARTS):
        at = PARTS * TILES + part
        norm = jnp.where(row >= part * TILES, jnp.sum(total[at : at + 1, :]), norm)
    new = jnp.where(row < PARTS * TILES, before * total / norm, 0.0)
    for peer in range(peers):
        out_ref[peer * PIECE : (peer + 1) * PIECE, :] = new


def update(axis, got, old):
    return pl.pallas_call(
        functools.partial(update_kernel, axis, got.shape[0] // PIECE),
        out_shape=jax.ShapeDtypeStruct(got.shape, F32),
        in_specs=[VMEM, VMEM],
        out_specs=VMEM,
        scratch_shapes=[pltpu.VMEM((PIECE, LANES), F32)],
        compiler_params=pltpu.CompilerParams(vmem_limit_bytes=4 * 2**20),
        name="update",
    )(got, old[0])


def whole_kernel(in_ref, out_ref):
    for part in range(PARTS):
        for tile in range(TILES):
            at = slice(tile * LANES, (tile + 1) * LANES)
            out_ref[part * PART : (part + 1) * PART, at] = load_tile([in_ref], None, part, tile)


def whole(pieces):
    return pl.pallas_call(
        whole_kernel,
        out_shape=jax.ShapeDtypeStruct((RANK, TILES * LANES), F32),
        in_specs=[VMEM],
        out_specs=VMEM,
        compiler_params=pltpu.CompilerParams(vmem_limit_bytes=4 * 2**20),
        name="whole",
    )(pieces)


def body(n_col, flow, anchor, destination):
    pairs = [(i, i ^ 1) for i in range(n_col)]
    cores = [list(range(core, n_col, 2)) for core in range(2)]

    def over_row(x):
        return lax.all_to_all(x, "row", 0, 0, tiled=True)

    def over_chips(x):
        return lax.all_to_all(x, "col", 0, 0, axis_index_groups=cores, tiled=True)

    def to_other_core(x):
        return lax.ppermute(x, "col", pairs)

    anchor, destination = (anchor,), (destination,)
    for sweep in range(ITERS):
        first, last = sweep == 0, sweep == ITERS - 1
        mine, other, *rest = half("anchor", flow, anchor, destination, first=first)
        if first:
            (flow,) = rest
        new = update("col", over_chips(mine + to_other_core(other)), anchor)
        mine = over_chips(new)
        anchor = (mine, to_other_core(mine))
        sent, *rest = half("destination", flow, destination, anchor, emit_v=last)
        destination = (over_row(update("row", over_row(sent), destination)),)
    return rest[0], whole(destination[0])


def solution(mesh):
    in_specs = (P("row", "col"), P(None, "row"), P(None, "col"))
    out_specs = (P(None, "row"), P(None, "col"))
    return jax.shard_map(
        functools.partial(body, mesh.shape["col"]),
        mesh=mesh,
        in_specs=in_specs,
        out_specs=out_specs,
        check_vma=False,
    )
```

```python
import functools

import jax
import jax.numpy as jnp
from jax import lax
from jax.experimental import pallas as pl
from jax.experimental.pallas import tpu as pltpu
from jax.sharding import PartitionSpec as P

ITERS = 2
RANK = 48
LANES = 128
COLS = 256
ROWS = 256
GROUP = 2

F32 = jnp.float32
BF16 = jnp.bfloat16

PART = 16
PARTS = RANK // PART

PIECE = 40
TILES = 12
VMEM = pl.BlockSpec(memory_space=pltpu.VMEM)


def split(x):
    high = x.astype(BF16)
    return high, (x - high.astype(F32)).astype(BF16)


def swap(core, mine, other):
    return jnp.where(core == 0, mine, other), jnp.where(core == 0, other, mine)


def load_tile(refs, core, part, tile):
    if refs[0].shape[0] == RANK:
        return refs[0][part * PART : (part + 1) * PART, tile * LANES : (tile + 1) * LANES]
    row = part * TILES + tile
    if len(refs) == 1:
        return refs[0][pl.ds(row, PART, stride=PIECE), :]
    half_part = [ref[pl.ds(row, PART // 2, stride=PIECE), :] for ref in refs]
    return jnp.concatenate(swap(core, *half_part), axis=0)


def store_rows(refs, core, row, x):
    if len(refs) == 1:
        refs[0][pl.ds(row, PART, stride=PIECE), :] = x
    else:
        for ref, y in zip(refs, swap(core, x[: PART // 2], x[PART // 2 :])):
            ref[pl.ds(row, PART // 2, stride=PIECE), :] = y


def half_kernel(kind, n_u, n_v, n_out, emit_v, first, *refs):
    refs = list(refs)
    take = lambda n: [refs.pop(0) for _ in range(n)]
    (flow_in,), u_refs, v_refs, out_refs = take(1), take(n_u), take(n_v), take(n_out)
    (v_out,) = take(1) if emit_v else (None,)
    (flow,) = take(1) if first else (flow_in,)
    v_t, v_cat, u_w, acc = take(4)
    zones_u, zones_v = u_w.shape[1], v_t.shape[0]
    steps = zones_u // COLS
    core = lax.rem(lax.axis_index("col"), 2)
    if emit_v:
        v_buf, emit_sem = refs
        emit = pltpu.make_async_copy(v_buf, v_out, emit_sem)

    def fetch(step):
        at = pl.ds(step * COLS, COLS)
        where = (at, slice(None)) if kind == "anchor" else (slice(None), at)
        return pltpu.make_async_copy(flow_in.at[where], flow.at[where], sem.at[step])

    if first:
        u_buf, v_buf, sem, factor_sem = refs
        copies = [
            pltpu.make_async_copy(u_refs[0], u_buf, factor_sem.at[0]),
            pltpu.make_async_copy(v_refs[0], v_buf, factor_sem.at[1]),
        ]
        for copy in copies:
            copy.start()
        for step in range(GROUP):
            fetch(step).start()
        for copy in copies:
            copy.wait()
        for step in range(GROUP, 2 * GROUP):
            fetch(step).start()
        u_refs, v_refs = [u_buf], [v_buf]

    gap = jnp.zeros((16, LANES), BF16)
    for tile in range(zones_u // LANES):
        at = slice(tile * LANES, (tile + 1) * LANES)
        for part in range(PARTS):
            low = part * PART
            for base, term in zip((0, 128), split(load_tile(u_refs, core, part, tile))):
                u_w[base + low : base + low + PART, at] = term
                u_w[base + 64 + low : base + 64 + low + PART, at] = term
        for base in (0, 64, 128, 192):
            u_w[base + RANK : base + 64, at] = gap
    sums = [None] * PARTS
    gap = gap.astype(F32)
    for tile in range(zones_v // LANES):
        at = slice(tile * LANES, (tile + 1) * LANES)
        heads, tails = [], []
        for part in range(PARTS):
            low = part * PART
            x = load_tile(v_refs, core, part, tile)
            high, low_term = split(x)
            v_cat[low : low + PART, at] = high
            v_cat[RANK + low : RANK + low + PART, at] = low_term
            heads.append(high.astype(F32))
            tails.append(low_term.astype(F32))
            sums[part] = x if tile == 0 else sums[part] + x
            if emit_v:
                v_buf[low : low + PART, at] = x
        x = jnp.concatenate([*heads, gap, *tails, gap], axis=0).T.astype(BF16)
        v_t[at, :LANES] = x
        v_t[at, LANES:] = x

    def slab(step):
        at = slice(step * COLS, (step + 1) * COLS)
        weights = u_w[:, at]
        total = None
        for block in range(zones_v // ROWS):
            rows = slice(block * ROWS, (block + 1) * ROWS)
            rebuilt = jnp.dot(v_t[rows, :], weights, preferred_element_type=F32)
            piece = flow[at, rows].T if kind == "anchor" else flow[rows, at]
            inverse = pl.reciprocal(rebuilt, approx=True)
            head = (piece * inverse).astype(BF16)
            tail = ((piece - rebuilt * head.astype(F32)) * inverse).astype(BF16)
            left = v_cat[:, rows]
            term = jnp.dot(left, head, preferred_element_type=F32)
            term += jnp.dot(left, tail, preferred_element_type=F32)
            total = term if total is None else total + term
        acc[:, at] = total[:RANK] + total[RANK:]

    for step in range(steps):
        if first and step % GROUP == 0:
            for landed in range(step, step + GROUP):
                fetch(landed).wait()
            for later in range(step + 2 * GROUP, min(step + 3 * GROUP, steps)):
                fetch(later).start()
        slab(step)
        if emit_v and step == 0:
            emit.start()
    if emit_v:
        emit.wait()

    for part in range(PARTS):
        ranks = slice(part * PART, (part + 1) * PART)
        for tile in range(TILES):
            x = acc[ranks, tile * LANES : (tile + 1) * LANES]
            store_rows(out_refs, core, part * TILES + tile, x)
        store_rows(out_refs, core, PARTS * TILES + part, sums[part])
    store_rows(out_refs, core, PARTS * TILES + PARTS, jnp.zeros((PART, LANES), F32))


def half(kind, flow, u, v, emit_v=False, first=False):
    zones_u, zones_v = flow.shape if kind == "anchor" else flow.shape[::-1]
    n_out = 2 if kind == "anchor" else 1
    out_shape = [jax.ShapeDtypeStruct((PART // n_out * PIECE, LANES), F32)] * n_out
    out_specs = [VMEM] * n_out
    if emit_v:
        out_shape.append(jax.ShapeDtypeStruct((RANK, zones_v), F32))
        out_specs.append(pl.BlockSpec(memory_space=pl.ANY))
    scratch = [
        pltpu.VMEM((zones_v, 2 * LANES), BF16),
        pltpu.VMEM((2 * RANK, zones_v), BF16),
        pltpu.VMEM((2 * LANES, zones_u), BF16),
        pltpu.VMEM((RANK, zones_u), F32),
    ]
    operands = [flow, *u, *v]
    if emit_v:
        scratch += [pltpu.VMEM((RANK, zones_v), F32), pltpu.SemaphoreType.DMA]
    if first:
        out_shape.append(pltpu.VMEM(flow.shape, F32))
        out_specs.append(VMEM)
        operands = [pltpu.with_memory_space_constraint(x, pltpu.HBM) for x in operands]
        scratch += [
            pltpu.VMEM((RANK, zones_u), F32),
            pltpu.VMEM((RANK, zones_v), F32),
            pltpu.SemaphoreType.DMA((zones_u // COLS,)),
            pltpu.SemaphoreType.DMA((2,)),
        ]
    return pl.pallas_call(
        functools.partial(half_kernel, kind, len(u), len(v), n_out, emit_v, first),
        out_shape=out_shape,
        in_specs=[pl.BlockSpec(memory_space=pl.ANY) if first else VMEM] * len(operands),
        out_specs=out_specs,
        scratch_shapes=scratch,
        compiler_params=pltpu.CompilerParams(vmem_limit_bytes=30 * 2**20),
        name="half_" + kind,
    )(*operands)


def update_kernel(axis, peers, got_ref, old_ref, out_ref, old):
    me = lax.axis_index(axis)
    if axis == "col":
        slot, core = me // 2, lax.rem(me, 2)
        me = core * (PART // 2) + slot
    else:
        slot = me
    if old_ref.shape[0] == RANK:
        for part in range(PARTS):
            x = old_ref[part * PART : (part + 1) * PART, :]
            mine = lax.broadcasted_iota(jnp.int32, x.shape, 0) == me
            x = jnp.sum(jnp.where(mine, x, 0.0), axis=0, keepdims=True)
            for tile in range(TILES):
                row = part * TILES + tile
                old[row : row + 1, :] = x[:, tile * LANES : (tile + 1) * LANES]
        old[PARTS * TILES :, :] = jnp.zeros((PIECE - PARTS * TILES, LANES), F32)
        before = old[...]
    else:
        before = old_ref[pl.ds(pl.multiple_of(slot * PIECE, 8), PIECE), :]
    total = got_ref[:PIECE, :]
    for peer in range(1, peers):
        total = total + got_ref[peer * PIECE : (peer + 1) * PIECE, :]
    row = lax.broadcasted_iota(jnp.int32, (PIECE, LANES), 0)
    norm = jnp.zeros((PIECE, LANES), F32)
    for part in range(PARTS):
        at = PARTS * TILES + part
        norm = jnp.where(row >= part * TILES, jnp.sum(total[at : at + 1, :]), norm)
    new = jnp.where(row < PARTS * TILES, before * total / norm, 0.0)
    for peer in range(peers):
        out_ref[peer * PIECE : (peer + 1) * PIECE, :] = new


def update(axis, got, old):
    return pl.pallas_call(
        functools.partial(update_kernel, axis, got.shape[0] // PIECE),
        out_shape=jax.ShapeDtypeStruct(got.shape, F32),
        in_specs=[VMEM, VMEM],
        out_specs=VMEM,
        scratch_shapes=[pltpu.VMEM((PIECE, LANES), F32)],
        compiler_params=pltpu.CompilerParams(vmem_limit_bytes=4 * 2**20),
        name="update",
    )(got, old[0])


def whole_kernel(in_ref, out_ref):
    for part in range(PARTS):
        for tile in range(TILES):
            at = slice(tile * LANES, (tile + 1) * LANES)
            out_ref[part * PART : (part + 1) * PART, at] = load_tile([in_ref], None, part, tile)


def whole(pieces):
    return pl.pallas_call(
        whole_kernel,
        out_shape=jax.ShapeDtypeStruct((RANK, TILES * LANES), F32),
        in_specs=[VMEM],
        out_specs=VMEM,
        compiler_params=pltpu.CompilerParams(vmem_limit_bytes=4 * 2**20),
        name="whole",
    )(pieces)


def body(n_col, flow, anchor, destination):
    pairs = [(i, i ^ 1) for i in range(n_col)]
    cores = [list(range(core, n_col, 2)) for core in range(2)]

    def over_row(x):
        return lax.all_to_all(x, "row", 0, 0, tiled=True)

    def over_chips(x):
        return lax.all_to_all(x, "col", 0, 0, axis_index_groups=cores, tiled=True)

    def to_other_core(x):
        return lax.ppermute(x, "col", pairs)

    anchor, destination = (anchor,), (destination,)
    for sweep in range(ITERS):
        first, last = sweep == 0, sweep == ITERS - 1
        mine, other, *rest = half("anchor", flow, anchor, destination, first=first)
        if first:
            (flow,) = rest
        new = update("col", over_chips(mine + to_other_core(other)), anchor)
        mine = over_chips(new)
        anchor = (mine, to_other_core(mine))
        sent, *rest = half("destination", flow, destination, anchor, emit_v=last)
        destination = (over_row(update("row", over_row(sent), destination)),)
    return rest[0], whole(destination[0])


def solution(mesh):
    in_specs = (P("row", "col"), P(None, "row"), P(None, "col"))
    out_specs = (P(None, "row"), P(None, "col"))
    return jax.shard_map(
        functools.partial(body, mesh.shape["col"]),
        mesh=mesh,
        in_specs=in_specs,
        out_specs=out_specs,
        check_vma=False,
    )
```

```python
import functools

import jax
import jax.numpy as jnp
from jax import lax
from jax.experimental import pallas as pl
from jax.experimental.pallas import tpu as pltpu
from jax.sharding import PartitionSpec as P

ITERS = 2
RANK = 48
LANES = 128
COLS = 256
ROWS = 256
HALF = 768

F32 = jnp.float32
BF16 = jnp.bfloat16
VMEM = pl.BlockSpec(memory_space=pltpu.VMEM)
ANY = pl.BlockSpec(memory_space=pl.ANY)

PIECE = 40
ROW_FORM = (16, 3, 12)
HALF_FORM = (8, 6, 6)
PART = 16


def split(x):
    high = x.astype(BF16)
    return high, (x - high.astype(F32)).astype(BF16)


def lanes(tile):
    return slice(tile * LANES, (tile + 1) * LANES)


def load_tile(ref, part, tile, base=None):
    ranks = slice(part * PART, (part + 1) * PART)
    if ref.shape[0] == RANK:
        at = lanes(tile) if base is None else pl.ds(pl.multiple_of(base + tile * LANES, LANES), LANES)
        return ref[ranks, at]
    if ref.shape[0] == ROW_FORM[0] * PIECE:
        return ref[pl.ds(part * ROW_FORM[2] + tile, 16, stride=PIECE), :]
    rows = [(2 * part + i) * HALF_FORM[2] + tile for i in range(2)]
    return jnp.concatenate([ref[pl.ds(row, 8, stride=PIECE), :] for row in rows], axis=0)


def store_pieces(ref, total, sums):
    pieces, ranks, tiles = ROW_FORM if ref.shape[0] == ROW_FORM[0] * PIECE else HALF_FORM
    for rank in range(ranks):
        for tile in range(tiles):
            x = total[rank * pieces : (rank + 1) * pieces, lanes(tile)]
            ref[pl.ds(rank * tiles + tile, pieces, stride=PIECE), :] = x
    for part, x in enumerate(sums):
        if pieces == 8:
            x = x + pltpu.roll(x, LANES // 2, 1)
            left = lax.broadcasted_iota(jnp.int32, (8, LANES), 1) < LANES // 2
            x = jnp.where(left, x[:8], x[8:])
        ref[pl.ds(ranks * tiles + part, pieces, stride=PIECE), :] = x
    ref[pl.ds(PIECE - 1, pieces, stride=PIECE), :] = jnp.zeros((pieces, LANES), F32)


def put_moving(u_ref, u_w, base=None):
    gap = jnp.zeros((16, LANES), BF16)
    for tile in range(u_w.shape[1] // LANES):
        at = lanes(tile)
        for part in range(3):
            low = part * PART
            for first, term in zip((0, 128), split(load_tile(u_ref, part, tile, base))):
                u_w[first + low : first + low + PART, at] = term
                u_w[first + 64 + low : first + 64 + low + PART, at] = term
        for first in (0, 64, 128, 192):
            u_w[first + RANK : first + 64, at] = gap


def put_fixed(v_ref, v_t, v_cat):
    sums = [None] * 3
    gap = jnp.zeros((16, LANES), F32)
    for tile in range(v_t.shape[0] // LANES):
        at = lanes(tile)
        heads, tails = [], []
        for part in range(3):
            low = part * PART
            x = load_tile(v_ref, part, tile)
            high, low_term = split(x)
            v_cat[low : low + PART, at] = high
            v_cat[RANK + low : RANK + low + PART, at] = low_term
            heads.append(high.astype(F32))
            tails.append(low_term.astype(F32))
            sums[part] = x if tile == 0 else sums[part] + x
        x = jnp.concatenate([*heads, gap, *tails, gap], axis=0).T.astype(BF16)
        v_t[at, :LANES] = x
        v_t[at, LANES:] = x
    return sums


def slab(flow, turned, v_t, v_cat, u_w, step):
    at = slice(step * COLS, (step + 1) * COLS)
    weights = u_w[:, at]
    total = None
    for block in range(v_t.shape[0] // ROWS):
        rows = slice(block * ROWS, (block + 1) * ROWS)
        rebuilt = jnp.dot(v_t[rows, :], weights, preferred_element_type=F32)
        piece = flow[at, rows].T if turned else flow[rows, at]
        inverse = pl.reciprocal(rebuilt, approx=True)
        head = (piece * inverse).astype(BF16)
        tail = ((piece - rebuilt * head.astype(F32)) * inverse).astype(BF16)
        left = v_cat[:, rows]
        term = jnp.dot(left, head, preferred_element_type=F32)
        term += jnp.dot(left, tail, preferred_element_type=F32)
        total = term if total is None else total + term
    return total[:RANK] + total[RANK:]


def anchor_kernel(mine, first, load, flow_in, u_ref, v_ref, out_ref, *refs):
    refs = list(refs)
    flow = refs.pop(0) if first else flow_in
    v_t, v_cat, u_w, acc = refs[:4]
    core = lax.rem(lax.axis_index("col"), 2)
    base = pl.multiple_of((core if mine else 1 - core) * HALF, HALF)
    steps = HALF // COLS
    if first:
        sem = refs[4]

        def fetch(step):
            there = pl.ds(pl.multiple_of(base + step * COLS, COLS), COLS)
            return pltpu.make_async_copy(
                flow_in.at[there, :], flow.at[step * COLS : (step + 1) * COLS, :], sem.at[step]
            )

        if load:
            u_buf, v_buf, factor_sem = refs[5:]
            copies = [
                pltpu.make_async_copy(u_ref, u_buf, factor_sem.at[0]),
                pltpu.make_async_copy(v_ref, v_buf, factor_sem.at[1]),
            ]
            for copy in copies:
                copy.start()
            u_ref, v_ref = u_buf, v_buf
        fetch(0).start()
        fetch(1).start()
        if load:
            for copy in copies:
                copy.wait()
        fetch(2).start()
    put_moving(u_ref, u_w, base if u_ref.shape[0] == RANK else None)
    sums = put_fixed(v_ref, v_t, v_cat)
    for step in range(steps):
        if first:
            fetch(step).wait()
        acc[:, step * COLS : (step + 1) * COLS] = slab(flow, True, v_t, v_cat, u_w, step)
    store_pieces(out_ref, acc, sums)


def cost(zones_u, zones_v):
    work = zones_u * zones_v
    return pl.CostEstimate(flops=1000 * work, bytes_accessed=4 * work, transcendentals=work)


def factor_scratch(zones_u, zones_v):
    return [
        pltpu.VMEM((zones_v, 2 * LANES), BF16),
        pltpu.VMEM((2 * RANK, zones_v), BF16),
        pltpu.VMEM((2 * LANES, zones_u), BF16),
        pltpu.VMEM((RANK, zones_u), F32),
    ]


def anchor_half(mine, flow, u, v, first=False):
    zones = flow.shape[1]
    load = first and not mine
    out_shape = [jax.ShapeDtypeStruct((HALF_FORM[0] * PIECE, LANES), F32)]
    scratch = factor_scratch(HALF, zones)
    in_specs = [VMEM] * 3
    if first:
        out_shape.append(pltpu.VMEM((HALF, zones), F32))
        scratch.append(pltpu.SemaphoreType.DMA((HALF // COLS,)))
        in_specs[0] = ANY
        flow = pltpu.with_memory_space_constraint(flow, pltpu.HBM)
    if load:
        in_specs = [ANY] * 3
        u, v = (pltpu.with_memory_space_constraint(x, pltpu.HBM) for x in (u, v))
        scratch += [pltpu.VMEM(u.shape, F32), pltpu.VMEM(v.shape, F32), pltpu.SemaphoreType.DMA((2,))]
    return pl.pallas_call(
        functools.partial(anchor_kernel, mine, first, load),
        out_shape=out_shape,
        in_specs=in_specs,
        out_specs=[VMEM] * len(out_shape),
        scratch_shapes=scratch,
        cost_estimate=cost(HALF, zones),
        compiler_params=pltpu.CompilerParams(vmem_limit_bytes=24 * 2**20),
        name="anchor_mine" if mine else "anchor_other",
    )(flow, u, v)


def near_kernel(flow, u_ref, v_ref, out_ref, v_t, v_cat, u_w):
    put_moving(u_ref, u_w)
    put_fixed(v_ref, v_t, v_cat)
    for step in range(u_w.shape[1] // COLS):
        out_ref[:, step * COLS : (step + 1) * COLS] = slab(flow, False, v_t, v_cat, u_w, step)


def far_kernel(emit, flow, u_ref, v_ref, near_ref, mine_ref, out_ref, *refs):
    refs = list(refs)
    v_out = refs.pop(0) if emit else None
    v_t, v_cat, u_w, acc = refs
    core = lax.rem(lax.axis_index("col"), 2)
    sums = put_fixed(v_ref, v_t, v_cat)
    for tile in range(HALF_FORM[2]):
        for part in range(3):
            x = load_tile(mine_ref, part, tile)
            sums[part] = sums[part] + x
            if emit:
                for y, owner in ((x, core), (load_tile(v_ref, part, tile), 1 - core)):
                    at = pl.ds(pl.multiple_of(owner * HALF + tile * LANES, LANES), LANES)
                    v_out[part * PART : (part + 1) * PART, at] = y
    put_moving(u_ref, u_w)
    for step in range(u_w.shape[1] // COLS):
        at = slice(step * COLS, (step + 1) * COLS)
        acc[:, at] = near_ref[:, at] + slab(flow, False, v_t, v_cat, u_w, step)
    store_pieces(out_ref, acc, sums)


def destination_half(flow_mine, flow_other, u, mine, other, emit):
    zones = flow_mine.shape[1]
    params = dict(
        cost_estimate=cost(zones, HALF),
        compiler_params=pltpu.CompilerParams(vmem_limit_bytes=24 * 2**20),
    )
    near = pl.pallas_call(
        near_kernel,
        out_shape=jax.ShapeDtypeStruct((RANK, zones), F32),
        in_specs=[VMEM] * 3,
        out_specs=VMEM,
        scratch_shapes=factor_scratch(zones, HALF)[:3],
        name="destination_near",
        **params,
    )(flow_mine, u, mine)
    out_shape = [jax.ShapeDtypeStruct((ROW_FORM[0] * PIECE, LANES), F32)]
    if emit:
        out_shape.append(jax.ShapeDtypeStruct((RANK, 2 * HALF), F32))
    return pl.pallas_call(
        functools.partial(far_kernel, emit),
        out_shape=out_shape,
        in_specs=[VMEM] * 5,
        out_specs=[VMEM] * len(out_shape),
        scratch_shapes=factor_scratch(zones, HALF),
        name="destination_far",
        **params,
    )(flow_other, u, other, near, mine)


def update_kernel(axis, got_ref, old_ref, out_ref, old):
    me = lax.axis_index(axis)
    pieces, ranks, tiles = ROW_FORM if axis == "row" else HALF_FORM
    if axis == "col":
        me, core = me // 2, lax.rem(me, 2)
    if old_ref.shape[0] == RANK:
        zones = slice(None) if axis == "row" else pl.ds(pl.multiple_of(core * HALF, HALF), HALF)
        for rank in range(ranks):
            x = old_ref[rank * pieces : (rank + 1) * pieces, zones]
            here = lax.broadcasted_iota(jnp.int32, x.shape, 0) == me
            x = jnp.sum(jnp.where(here, x, 0.0), axis=0, keepdims=True)
            for tile in range(tiles):
                row = rank * tiles + tile
                old[row : row + 1, :] = x[:, lanes(tile)]
        old[ranks * tiles :, :] = jnp.zeros((PIECE - ranks * tiles, LANES), F32)
        before = old[...]
    else:
        before = old_ref[pl.ds(pl.multiple_of(me * PIECE, 8), PIECE), :]
    total = got_ref[:PIECE, :]
    for peer in range(1, pieces):
        total = total + got_ref[peer * PIECE : (peer + 1) * PIECE, :]
    row = lax.broadcasted_iota(jnp.int32, (PIECE, LANES), 0)
    norm = jnp.zeros((PIECE, LANES), F32)
    for rank in range(ranks):
        at = ranks * tiles + (rank if axis == "row" else rank // 2)
        x = total[at : at + 1, :]
        if axis == "col":
            left = lax.broadcasted_iota(jnp.int32, x.shape, 1) < LANES // 2
            x = jnp.where(left, x, 0.0) if rank % 2 == 0 else jnp.where(left, 0.0, x)
        norm = jnp.where(row >= rank * tiles, jnp.sum(x), norm)
    new = jnp.where(row < ranks * tiles, before * total / norm, 0.0)
    for peer in range(pieces):
        out_ref[peer * PIECE : (peer + 1) * PIECE, :] = new


def update(axis, got, old):
    return pl.pallas_call(
        functools.partial(update_kernel, axis),
        out_shape=jax.ShapeDtypeStruct(got.shape, F32),
        in_specs=[VMEM, VMEM],
        out_specs=VMEM,
        scratch_shapes=[pltpu.VMEM((PIECE, LANES), F32)],
        compiler_params=pltpu.CompilerParams(vmem_limit_bytes=4 * 2**20),
        name="update",
    )(got, old)


def whole_kernel(in_ref, out_ref):
    for part in range(3):
        for tile in range(ROW_FORM[2]):
            out_ref[part * PART : (part + 1) * PART, lanes(tile)] = load_tile(in_ref, part, tile)


def whole(pieces):
    return pl.pallas_call(
        whole_kernel,
        out_shape=jax.ShapeDtypeStruct((RANK, ROW_FORM[2] * LANES), F32),
        in_specs=[VMEM],
        out_specs=VMEM,
        compiler_params=pltpu.CompilerParams(vmem_limit_bytes=4 * 2**20),
        name="whole",
    )(pieces)


def body(n_col, flow, anchor, destination):
    pairs = [(i, i ^ 1) for i in range(n_col)]
    cores = [list(range(core, n_col, 2)) for core in range(2)]

    def over_row(x):
        return lax.all_to_all(x, "row", 0, 0, tiled=True)

    def over_chips(x):
        return lax.all_to_all(x, "col", 0, 0, axis_index_groups=cores, tiled=True)

    def to_other(x):
        return lax.ppermute(x, "col", pairs)

    mine, other, flow_mine, flow_other = anchor, anchor, flow, flow
    for sweep in range(ITERS):
        first, last = sweep == 0, sweep == ITERS - 1
        sent, *rest = anchor_half(False, flow_other, other, destination, first)
        flow_other = rest[0] if first else flow_other
        got = to_other(sent)
        sent, *rest = anchor_half(True, flow_mine, mine, destination, first)
        flow_mine = rest[0] if first else flow_mine
        mine = over_chips(update("col", over_chips(sent + got), mine))
        other = to_other(mine)
        sent, *rest = destination_half(flow_mine, flow_other, destination, mine, other, last)
        destination = over_row(update("row", over_row(sent), destination))
    return rest[0], whole(destination)


def solution(mesh):
    in_specs = (P("row", "col"), P(None, "row"), P(None, "col"))
    out_specs = (P(None, "row"), P(None, "col"))
    return jax.shard_map(
        functools.partial(body, mesh.shape["col"]),
        mesh=mesh,
        in_specs=in_specs,
        out_specs=out_specs,
        check_vma=False,
    )
```

```python
import functools

import jax
import jax.numpy as jnp
from jax import lax
from jax.experimental import pallas as pl
from jax.experimental.pallas import tpu as pltpu
from jax.sharding import PartitionSpec as P

ITERS = 2
RANK = 48
LANES = 128
COLS = 256
ROWS = 256
HALF = 768

F32 = jnp.float32
BF16 = jnp.bfloat16
VMEM = pl.BlockSpec(memory_space=pltpu.VMEM)
ANY = pl.BlockSpec(memory_space=pl.ANY)

PIECE = 40
ROW_FORM = (16, 3, 12)
HALF_FORM = (8, 6, 6)
PART = 16


def split(x):
    high = x.astype(BF16)
    return high, (x - high.astype(F32)).astype(BF16)


def lanes(tile):
    return slice(tile * LANES, (tile + 1) * LANES)


def load_tile(ref, part, tile, base=None):
    ranks = slice(part * PART, (part + 1) * PART)
    if ref.shape[0] == RANK:
        at = lanes(tile) if base is None else pl.ds(pl.multiple_of(base + tile * LANES, LANES), LANES)
        return ref[ranks, at]
    if ref.shape[0] == ROW_FORM[0] * PIECE:
        return ref[pl.ds(part * ROW_FORM[2] + tile, 16, stride=PIECE), :]
    rows = [(2 * part + i) * HALF_FORM[2] + tile for i in range(2)]
    return jnp.concatenate([ref[pl.ds(row, 8, stride=PIECE), :] for row in rows], axis=0)


def store_pieces(ref, total, sums):
    pieces, ranks, tiles = ROW_FORM if ref.shape[0] == ROW_FORM[0] * PIECE else HALF_FORM
    for rank in range(ranks):
        for tile in range(tiles):
            x = total[rank * pieces : (rank + 1) * pieces, lanes(tile)]
            ref[pl.ds(rank * tiles + tile, pieces, stride=PIECE), :] = x
    for part, x in enumerate(sums):
        if pieces == 8:
            x = x + pltpu.roll(x, LANES // 2, 1)
            left = lax.broadcasted_iota(jnp.int32, (8, LANES), 1) < LANES // 2
            x = jnp.where(left, x[:8], x[8:])
        ref[pl.ds(ranks * tiles + part, pieces, stride=PIECE), :] = x
    ref[pl.ds(PIECE - 1, pieces, stride=PIECE), :] = jnp.zeros((pieces, LANES), F32)


def put_moving(u_ref, u_w, base=None):
    gap = jnp.zeros((16, LANES), BF16)
    for tile in range(u_w.shape[1] // LANES):
        at = lanes(tile)
        for part in range(3):
            low = part * PART
            for first, term in zip((0, 128), split(load_tile(u_ref, part, tile, base))):
                u_w[first + low : first + low + PART, at] = term
                u_w[first + 64 + low : first + 64 + low + PART, at] = term
        for first in (0, 64, 128, 192):
            u_w[first + RANK : first + 64, at] = gap


def put_fixed(v_ref, v_t, v_cat):
    sums = [None] * 3
    gap = jnp.zeros((16, LANES), F32)
    for tile in range(v_t.shape[0] // LANES):
        at = lanes(tile)
        heads, tails = [], []
        for part in range(3):
            low = part * PART
            x = load_tile(v_ref, part, tile)
            high, low_term = split(x)
            v_cat[low : low + PART, at] = high
            v_cat[RANK + low : RANK + low + PART, at] = low_term
            heads.append(high.astype(F32))
            tails.append(low_term.astype(F32))
            sums[part] = x if tile == 0 else sums[part] + x
        x = jnp.concatenate([*heads, gap, *tails, gap], axis=0).T.astype(BF16)
        v_t[at, :LANES] = x
        v_t[at, LANES:] = x
    return sums


def slab(flow, turned, v_t, v_cat, u_w, step):
    at = slice(step * COLS, (step + 1) * COLS)
    weights = u_w[:, at]
    total = None
    for block in range(v_t.shape[0] // ROWS):
        rows = slice(block * ROWS, (block + 1) * ROWS)
        rebuilt = jnp.dot(v_t[rows, :], weights, preferred_element_type=F32)
        piece = flow[at, rows].T if turned else flow[rows, at]
        inverse = pl.reciprocal(rebuilt, approx=True)
        head = (piece * inverse).astype(BF16)
        tail = ((piece - rebuilt * head.astype(F32)) * inverse).astype(BF16)
        left = v_cat[:, rows]
        term = jnp.dot(left, head, preferred_element_type=F32)
        term += jnp.dot(left, tail, preferred_element_type=F32)
        total = term if total is None else total + term
    return total[:RANK] + total[RANK:]


def anchor_kernel(mine, first, flow_in, u_ref, v_ref, out_ref, *refs):
    refs = list(refs)
    flow, flow_next = (refs.pop(0), refs.pop(0)) if first else (flow_in, None)
    v_t, v_cat, u_w, acc = refs[:4]
    core = lax.rem(lax.axis_index("col"), 2)
    owner = core if mine else 1 - core
    base = pl.multiple_of(owner * HALF, HALF)
    steps = HALF // COLS

    def fetch(step):
        half, into = (owner, flow) if step < steps else (1 - owner, flow_next)
        low = step % steps * COLS
        there = pl.ds(pl.multiple_of(half * HALF + low, COLS), COLS)
        return pltpu.make_async_copy(flow_in.at[there, :], into.at[low : low + COLS, :], sem.at[step])

    if first:
        sem, u_buf, v_buf, factor_sem = refs[4:]
        copies = [
            pltpu.make_async_copy(u_ref, u_buf, factor_sem.at[0]),
            pltpu.make_async_copy(v_ref, v_buf, factor_sem.at[1]),
        ]
        for copy in copies:
            copy.start()
        fetch(0).start()
        fetch(1).start()
        for copy in copies:
            copy.wait()
        fetch(2).start()
        u_ref, v_ref = u_buf, v_buf
    put_moving(u_ref, u_w, base if u_ref.shape[0] == RANK else None)
    sums = put_fixed(v_ref, v_t, v_cat)
    for step in range(steps):
        if first:
            fetch(step).wait()
            fetch(step + 3).start()
        acc[:, step * COLS : (step + 1) * COLS] = slab(flow, True, v_t, v_cat, u_w, step)
    store_pieces(out_ref, acc, sums)
    if first:
        for step in range(steps, 2 * steps):
            fetch(step).wait()


def cost(zones_u, zones_v):
    work = zones_u * zones_v
    return pl.CostEstimate(flops=1000 * work, bytes_accessed=4 * work, transcendentals=work)


def factor_scratch(zones_u, zones_v):
    return [
        pltpu.VMEM((zones_v, 2 * LANES), BF16),
        pltpu.VMEM((2 * RANK, zones_v), BF16),
        pltpu.VMEM((2 * LANES, zones_u), BF16),
        pltpu.VMEM((RANK, zones_u), F32),
    ]


def anchor_half(mine, flow, u, v, first=False):
    zones = flow.shape[1]
    out_shape = [jax.ShapeDtypeStruct((HALF_FORM[0] * PIECE, LANES), F32)]
    scratch = factor_scratch(HALF, zones)
    operands = [flow, u, v]
    if first:
        out_shape += [pltpu.VMEM((HALF, zones), F32)] * 2
        operands = [pltpu.with_memory_space_constraint(x, pltpu.HBM) for x in operands]
        scratch += [
            pltpu.SemaphoreType.DMA((2 * HALF // COLS,)),
            pltpu.VMEM(u.shape, F32),
            pltpu.VMEM(v.shape, F32),
            pltpu.SemaphoreType.DMA((2,)),
        ]
    return pl.pallas_call(
        functools.partial(anchor_kernel, mine, first),
        out_shape=out_shape,
        in_specs=[ANY if first else VMEM] * 3,
        out_specs=[VMEM] * len(out_shape),
        scratch_shapes=scratch,
        cost_estimate=cost(HALF, zones),
        compiler_params=pltpu.CompilerParams(vmem_limit_bytes=24 * 2**20),
        name="anchor_mine" if mine else "anchor_other",
    )(*operands)


def near_kernel(flow, u_ref, v_ref, out_ref, v_t, v_cat, u_w):
    put_moving(u_ref, u_w)
    put_fixed(v_ref, v_t, v_cat)
    for step in range(u_w.shape[1] // COLS):
        out_ref[:, step * COLS : (step + 1) * COLS] = slab(flow, False, v_t, v_cat, u_w, step)


def far_kernel(flow, u_ref, v_ref, near_ref, mine_ref, out_ref, v_t, v_cat, u_w, acc):
    sums = put_fixed(v_ref, v_t, v_cat)
    for tile in range(HALF_FORM[2]):
        for part in range(3):
            sums[part] = sums[part] + load_tile(mine_ref, part, tile)
    put_moving(u_ref, u_w)
    for step in range(u_w.shape[1] // COLS):
        at = slice(step * COLS, (step + 1) * COLS)
        acc[:, at] = near_ref[:, at] + slab(flow, False, v_t, v_cat, u_w, step)
    store_pieces(out_ref, acc, sums)


def destination_half(flow_mine, flow_other, u, mine, other):
    zones = flow_mine.shape[1]
    params = dict(
        cost_estimate=cost(zones, HALF),
        compiler_params=pltpu.CompilerParams(vmem_limit_bytes=24 * 2**20),
    )
    near = pl.pallas_call(
        near_kernel,
        out_shape=jax.ShapeDtypeStruct((RANK, zones), F32),
        in_specs=[VMEM] * 3,
        out_specs=VMEM,
        scratch_shapes=factor_scratch(zones, HALF)[:3],
        name="destination_near",
        **params,
    )(flow_mine, u, mine)
    return pl.pallas_call(
        far_kernel,
        out_shape=jax.ShapeDtypeStruct((ROW_FORM[0] * PIECE, LANES), F32),
        in_specs=[VMEM] * 5,
        out_specs=VMEM,
        scratch_shapes=factor_scratch(zones, HALF),
        name="destination_far",
        **params,
    )(flow_other, u, other, near, mine)


def update_kernel(axis, got_ref, old_ref, out_ref, old):
    me = lax.axis_index(axis)
    pieces, ranks, tiles = ROW_FORM if axis == "row" else HALF_FORM
    if axis == "col":
        me, core = me // 2, lax.rem(me, 2)
    if old_ref.shape[0] == RANK:
        zones = slice(None) if axis == "row" else pl.ds(pl.multiple_of(core * HALF, HALF), HALF)
        for rank in range(ranks):
            x = old_ref[rank * pieces : (rank + 1) * pieces, zones]
            here = lax.broadcasted_iota(jnp.int32, x.shape, 0) == me
            x = jnp.sum(jnp.where(here, x, 0.0), axis=0, keepdims=True)
            for tile in range(tiles):
                row = rank * tiles + tile
                old[row : row + 1, :] = x[:, lanes(tile)]
        old[ranks * tiles :, :] = jnp.zeros((PIECE - ranks * tiles, LANES), F32)
        before = old[...]
    else:
        before = old_ref[pl.ds(pl.multiple_of(me * PIECE, 8), PIECE), :]
    total = got_ref[:PIECE, :]
    for peer in range(1, pieces):
        total = total + got_ref[peer * PIECE : (peer + 1) * PIECE, :]
    row = lax.broadcasted_iota(jnp.int32, (PIECE, LANES), 0)
    norm = jnp.zeros((PIECE, LANES), F32)
    for rank in range(ranks):
        at = ranks * tiles + (rank if axis == "row" else rank // 2)
        x = total[at : at + 1, :]
        if axis == "col":
            left = lax.broadcasted_iota(jnp.int32, x.shape, 1) < LANES // 2
            x = jnp.where(left, x, 0.0) if rank % 2 == 0 else jnp.where(left, 0.0, x)
        norm = jnp.where(row >= rank * tiles, jnp.sum(x), norm)
    new = jnp.where(row < ranks * tiles, before * total / norm, 0.0)
    for peer in range(pieces):
        out_ref[peer * PIECE : (peer + 1) * PIECE, :] = new


def update(axis, got, old):
    return pl.pallas_call(
        functools.partial(update_kernel, axis),
        out_shape=jax.ShapeDtypeStruct(got.shape, F32),
        in_specs=[VMEM, VMEM],
        out_specs=VMEM,
        scratch_shapes=[pltpu.VMEM((PIECE, LANES), F32)],
        compiler_params=pltpu.CompilerParams(vmem_limit_bytes=4 * 2**20),
        name="update",
    )(got, old)


def whole_kernel(mine_ref, other_ref, in_ref, anchor_out, destination_out):
    core = lax.rem(lax.axis_index("col"), 2)
    for part in range(3):
        ranks = slice(part * PART, (part + 1) * PART)
        for tile in range(ROW_FORM[2]):
            destination_out[ranks, lanes(tile)] = load_tile(in_ref, part, tile)
        for ref, owner in ((mine_ref, core), (other_ref, 1 - core)):
            for tile in range(HALF_FORM[2]):
                at = pl.ds(pl.multiple_of(owner * HALF + tile * LANES, LANES), LANES)
                anchor_out[ranks, at] = load_tile(ref, part, tile)


def whole(mine, other, pieces):
    shape = jax.ShapeDtypeStruct((RANK, 2 * HALF), F32)
    return pl.pallas_call(
        whole_kernel,
        out_shape=[shape, shape],
        in_specs=[VMEM] * 3,
        out_specs=[VMEM] * 2,
        compiler_params=pltpu.CompilerParams(vmem_limit_bytes=4 * 2**20),
        name="whole",
    )(mine, other, pieces)


def body(n_col, flow, anchor, destination):
    pairs = [(i, i ^ 1) for i in range(n_col)]
    cores = [list(range(core, n_col, 2)) for core in range(2)]

    def over_row(x):
        return lax.all_to_all(x, "row", 0, 0, tiled=True)

    def over_chips(x):
        return lax.all_to_all(x, "col", 0, 0, axis_index_groups=cores, tiled=True)

    def to_other(x):
        return lax.ppermute(x, "col", pairs)

    mine, other, flow_mine, flow_other = anchor, anchor, flow, flow
    for sweep in range(ITERS):
        first = sweep == 0
        sent, *rest = anchor_half(False, flow_other, other, destination, first)
        if first:
            flow_other, flow_mine = rest
        got = to_other(sent)
        (sent,) = anchor_half(True, flow_mine, mine, destination)
        mine = over_chips(update("col", over_chips(sent + got), mine))
        other = to_other(mine)
        sent = destination_half(flow_mine, flow_other, destination, mine, other)
        destination = over_row(update("row", over_row(sent), destination))
    return tuple(whole(mine, other, destination))


def solution(mesh):
    in_specs = (P("row", "col"), P(None, "row"), P(None, "col"))
    out_specs = (P(None, "row"), P(None, "col"))
    return jax.shard_map(
        functools.partial(body, mesh.shape["col"]),
        mesh=mesh,
        in_specs=in_specs,
        out_specs=out_specs,
        check_vma=False,
    )
```
